32 devices in a mesh: layer: 2 (over core), feat: 8 (over z, x), dp: 2 (over y).
Axes of the slice: x: 2, y: 2, z: 4, core: 2. Of those that a mesh axis runs over, the one named last changes fastest.
Arguments:
- resid: bfloat16 [2, 256, 1792], P('layer', 'dp', 'feat'), may hold values from -6 to 6
- target: bfloat16 [2, 256, 1792], P('layer', 'feat', 'dp'), may hold values from -6 to 6
- enc_weight: bfloat16 [2, 1792, 4096], P('layer', None, 'feat'), may hold values from -6 to 6
- enc_bias: float32 [2, 4096], P('layer', 'feat'), may hold values from -3 to 3
- dec_weight: bfloat16 [2, 2, 4096, 1792], P('layer', None, 'feat', 'dp'), may hold values from -6 to 6
- dec_bias: float32 [2, 1792], P('layer', 'dp'), may hold values from -3 to 3
Outputs:
- new_enc_weight: bfloat16 [2, 1792, 4096], P('layer', 'dp', 'feat')
- new_enc_bias: float32 [2, 4096], P('layer', 'feat')
- new_dec_weight: bfloat16 [2, 2, 4096, 1792], P('layer', None, 'feat', 'dp')
- new_dec_bias: float32 [2, 1792], P('layer', 'dp')
The draws below stay inside these ranges and needn't reach their ends.
All inputs are finite; a program needn't handle non-finite values.
Results may differ from the reference program's by a relative error of at most 0.0065.
Values may be sent and summed in bfloat16 or wider, within the bound.
No kernel may reach another device: no remote copies, remote signals or barrier semaphores. Data moves between devices by JAX's collectives and lax.ppermute only.
A program may use at most 64 MiB of HBM per device.

```python
import jax
import jax.numpy as jnp

D = 1792
F = 4096
LAYERS = 2
ROWS = 256


def shard_levels(key, extent, shards, smallest, top_value):
    def one(position, shards_of):
        draws = jax.random.uniform(jax.random.fold_in(jax.random.fold_in(key, 6), position), (shards_of,), jnp.float32, smallest / len(shards), top_value / len(shards))
        return jnp.repeat(jnp.exp(draws), extent[position] // shards_of).reshape((-1,) + (1,) * (len(extent) - position - 1))

    factor_of = one(*shards[0])
    for cut in shards[1:]:
        factor_of = factor_of * one(*cut)
    return factor_of


def centred(own_key, dims, width, reach, cuts=(), dtype=jnp.bfloat16):
    entries = width * jax.random.normal(own_key, dims, jnp.float32)
    if cuts:
        entries = entries * shard_levels(own_key, dims, cuts, -0.22, 0.18)
    return jnp.clip(entries, -reach, reach).astype(dtype)


def setup_inputs(seed: int = 0) -> dict:
    streams_of = jax.random.split(jax.random.key(seed), 7)
    resid = centred(streams_of[0], (LAYERS, ROWS, D), 1.0, 6.0, ((0, 2), (1, 2), (2, 8)))
    target = centred(streams_of[1], (LAYERS, ROWS, D), 1.0, 6.0, ((0, 2), (1, 8), (2, 2)))
    enc_weight = centred(streams_of[2], (LAYERS, D, F), 1.0, 6.0, ((0, 2), (2, 8)))
    enc_bias = centred(streams_of[3], (LAYERS, F), 0.5, 3.0, ((0, 2), (1, 8)), jnp.float32)
    dec_weight = centred(streams_of[4], (LAYERS, LAYERS, F, D), 1.0, 6.0, ((0, 2), (2, 8), (3, 2)))
    dec_bias = centred(streams_of[5], (LAYERS, D), 0.5, 3.0, ((0, 2), (1, 2)), jnp.float32)
    return dict(resid=resid, target=target, enc_weight=enc_weight, enc_bias=enc_bias, dec_weight=dec_weight, dec_bias=dec_bias)


step_weight = 256.0
step_bias = 4.0


def reference(resid, target, enc_weight, enc_bias, dec_weight, dec_bias):
    layer_count = resid.shape[0]
    row_count = resid.shape[1]
    enc_scale = D ** -0.5
    dec_scale = F ** -0.5
    scale_rows = dec_scale / row_count
    codes = []
    preacts = []
    for source in range(layer_count):
        preact = enc_scale * jnp.dot(resid[source], enc_weight[source], preferred_element_type=jnp.float32) + enc_bias[source]
        preacts.append(preact)
        codes.append(jnp.maximum(preact, 0.0).astype(jnp.bfloat16))
    errors = []
    new_dec_bias = []
    for sink in range(layer_count):
        total = jnp.zeros((row_count, D), jnp.float32)
        for source in range(sink + 1):
            total = total + jnp.dot(codes[source], dec_weight[sink, source], preferred_element_type=jnp.float32)
        recon = dec_scale * total + dec_bias[sink]
        error_now = (recon - target[sink].astype(jnp.float32)).astype(jnp.bfloat16)
        errors.append(error_now)
        new_dec_bias.append(dec_bias[sink] - step_bias * jnp.sum(error_now.astype(jnp.float32), axis=0) / row_count)
    new_rows = []
    for sink in range(layer_count):
        blocks = []
        for source in range(layer_count):
            if source <= sink:
                grad_block = scale_rows * jnp.dot(codes[source].T, errors[sink], preferred_element_type=jnp.float32)
                blocks.append((dec_weight[sink, source].astype(jnp.float32) - step_weight * grad_block).astype(jnp.bfloat16))
            else:
                blocks.append(dec_weight[sink, source])
        new_rows.append(jnp.stack(blocks))
    new_dec_weight = jnp.stack(new_rows)
    new_enc = []
    new_enc_bias = []
    for source in range(layer_count):
        total = jnp.zeros((row_count, F), jnp.float32)
        for sink in range(source, layer_count):
            total = total + jnp.dot(errors[sink], dec_weight[sink, source].T, preferred_element_type=jnp.float32)
        code_grad = scale_rows * total
        pre_grad = jnp.where(preacts[source] > 0.0, code_grad, jnp.zeros_like(code_grad)).astype(jnp.bfloat16)
        enc_grad = enc_scale * jnp.dot(resid[source].T, pre_grad, preferred_element_type=jnp.float32)
        new_enc.append((enc_weight[source].astype(jnp.float32) - step_weight * enc_grad).astype(jnp.bfloat16))
        new_enc_bias.append(enc_bias[source] - step_bias * jnp.sum(pre_grad.astype(jnp.float32), axis=0))
    return jnp.stack(new_enc), jnp.stack(new_enc_bias), new_dec_weight, jnp.stack(new_dec_bias)
```

```python
import functools

import jax
import jax.numpy as jnp
from jax import lax
from jax.experimental import pallas as pl
from jax.experimental.pallas import tpu as pltpu
from jax.sharding import PartitionSpec as P

step_weight = 256.0
step_bias = 4.0
bf16 = jnp.bfloat16
f32 = jnp.float32


def contract_rows(left, right):
    return lax.dot_general(
        left, right, (((0,), (0,)), ((), ())), preferred_element_type=jnp.float32
    )


def contract_width(left, right):
    return lax.dot_general(
        left, right, (((1,), (1,)), ((), ())), preferred_element_type=jnp.float32
    )


def dot(left, right):
    return jnp.dot(left, right, preferred_element_type=jnp.float32)


def call(body, name, out_shape, *operands):
    return pl.pallas_call(body, out_shape=out_shape, name=name)(*operands)


def near(low):
    return range(4) if low else range(1, 4)


def swap_feat(value, mask):
    count = lax.axis_size("feat")
    return lax.ppermute(value, "feat", [(i, i ^ mask) for i in range(count)])


def swap_dp(value):
    return lax.ppermute(value, "dp", [(0, 1), (1, 0)])


def aligned(i, size):
    return pl.ds(pl.multiple_of(i * size, size), size)


def encode_body(scale, near0, near1, near2, near3, weight, bias, codes, halves):
    feat = lax.axis_index("feat")
    dp = lax.axis_index("dp")
    far, _, depth = near0.shape
    own_first = far // 2 * ((feat // (2 * far) + 1 - dp) % 2)
    total = None
    for s, blocks in enumerate((near0, near1, near2, near3)):
        for t in range(far):
            source = feat ^ (s + 4 * t)
            part = dot(blocks[t], weight[0, aligned(source, depth), :])
            total = part if total is None else total + part
        for u in range(far // 2):
            halves[s, u] = blocks[own_first + u]
    codes[...] = jnp.maximum(scale * total + bias[...], 0.0).astype(bf16)


def decode_body(scale, layers, *refs):
    own, partner = refs[:2]
    from_own = refs[2 : 1 + layers]
    from_partner = refs[1 + layers : 2 * layers]
    weight = refs[2 * layers]
    keep, send1, send2, send3, stacked, total = refs[2 * layers + 1 :]
    layer = lax.axis_index("layer")
    quarter = lax.axis_index("feat") % 4
    rows = own.shape[0]
    for half, parts in enumerate(((own, *from_own), (partner, *from_partner))):
        result = None
        for shift, codes in enumerate(parts):
            stacked[shift, half * rows : (half + 1) * rows, :] = codes[...]
            source = (layer + layers - shift) % layers
            part = dot(codes[...], weight[0, source])
            result = part if result is None else result + part
        total[...] = scale * result
        _, groups, block, _ = keep.shape
        for g in range(groups):
            keep[half, g] = total[aligned(4 * g + quarter, block), :]
            for s, send in ((1, send1), (2, send2), (3, send3)):
                send[half, g] = total[aligned(4 * g + (quarter ^ s), block), :].astype(bf16)


def add_body(keep, one, two, three, out):
    out[...] = (
        (keep[...] + one[...].astype(f32)) + (two[...].astype(f32) + three[...].astype(f32))
    ).astype(bf16)


def error_body(first, second, targets, bias, errors):
    far_own = lax.axis_index("feat") // 4
    dp = lax.axis_index("dp")
    _, groups, _, _ = first.shape
    for half in range(2):
        for g in range(groups):
            far = (dp ^ half) * groups + g
            recon = first[half, g].astype(f32) + second[half, g].astype(f32) + bias[...]
            errors[half, g] = (recon - targets[far ^ far_own].astype(f32)).astype(bf16)


def back_body(scale, rate, layers, *refs):
    near_errors = refs[:4]
    weight, bias = refs[4:6]
    errors, new_bias = refs[6:8]
    terms = refs[8:]
    layer = lax.axis_index("layer")
    quarter = lax.axis_index("feat") % 4
    _, groups, block, _ = near_errors[0].shape
    for half in range(2):
        for g in range(groups):
            for s, source in enumerate(near_errors):
                errors[aligned((half * groups + g) * 4 + (quarter ^ s), block), :] = source[half, g]
    value = errors[...]
    for shift, term in enumerate(terms, 1):
        source = (layer + layers - shift) % layers
        term[...] = (scale * contract_width(value, weight[0, source])).astype(bf16)
    new_bias[...] = bias[...] - rate * jnp.sum(value.astype(f32), axis=0, keepdims=True)


def own_body(scale, layers, errors, weight, *refs):
    total = scale * contract_width(errors[...], weight[0, lax.axis_index("layer")])
    for received in refs[:-1]:
        total = total + received[...].astype(f32)
    refs[-1][...] = total.astype(bf16)


def decoder_body(scale, layers, stacked, errors, weight, new_weight):
    layer = lax.axis_index("layer")
    shift = (layer + layers - pl.program_id(0)) % layers
    columns = pl.program_id(1)
    width = new_weight.shape[2]
    codes = stacked[shift, :, aligned(columns, width)] if False else stacked[shift]
    grad = contract_rows(codes, errors[...])
    new_weight[0, 0] = (weight[0, 0].astype(f32) - scale * grad).astype(bf16)


def encoder_body(
    scale, near0, near1, near2, near3, others, codes, term, other_term, weight, bias, new_weight,
    new_bias
):
    feat = lax.axis_index("feat")
    dp = lax.axis_index("dp")
    far, rows, depth = near0.shape
    first = far // 2 * ((feat // (2 * far) + dp) % 2)
    grads = []
    sums = []
    for half in range(2):
        mine = slice(half * rows, (half + 1) * rows)
        theirs = slice((1 - half) * rows, (2 - half) * rows)
        summed = term[mine, :].astype(f32) + other_term[theirs, :].astype(f32)
        alive = codes[0, mine, :].astype(f32) > 0.0
        grad = jnp.where(alive, summed, 0.0).astype(bf16)
        grads.append(grad)
        sums.append(jnp.sum(grad.astype(f32), axis=0, keepdims=True))
    new_bias[...] = bias[...] - step_bias * (sums[0] + sums[1])
    for s, blocks in enumerate((near0, near1, near2, near3)):
        for u in range(far // 2):
            grad = contract_rows(blocks[first + u], grads[0]) + contract_rows(others[s, u], grads[1])
            source = (feat ^ (s + 4 * u)) % (2 * far)
            old = weight[0, aligned(dp * 2 * far + source, depth), :]
            new_weight[0, aligned(source, depth), :] = (old.astype(f32) - scale * grad).astype(bf16)


def shape(dims, dtype):
    return jax.ShapeDtypeStruct(dims, dtype)


def exchange(resid, target, enc_weight, enc_bias, dec_weight, dec_bias):
    layers = lax.axis_size("layer")
    count = lax.axis_size("feat")
    _, rows, depth = resid.shape
    _, width, feat_dev = enc_weight.shape
    half_width = dec_weight.shape[3]
    row_count = rows * lax.axis_size("dp")
    far = count // 4
    block = row_count // count
    enc_scale = width ** (-0.5)
    dec_scale = (feat_dev * count) ** (-0.5)
    scale_rows = dec_scale / row_count

    near0 = resid
    targets = target
    bit = 4
    while bit < count:
        near0 = jnp.concatenate([near0, swap_feat(near0, bit)])
        bit *= 2
    inputs = [near0] + [swap_feat(near0, s) for s in range(1, 4)]
    codes, halves = call(
        functools.partial(encode_body, enc_scale),
        "encode",
        (shape((rows, feat_dev), bf16), shape((4, far // 2, rows, depth), bf16)),
        *inputs, enc_weight, enc_bias,
    )
    bit = 4
    while bit < count:
        targets = jnp.concatenate([targets, swap_feat(targets, bit)])
        bit *= 2

    def to_later(value, shift):
        return lax.ppermute(value, "layer", [(i, i + shift) for i in range(layers - shift)])

    partner = swap_dp(codes)
    from_own = [to_later(codes, shift) for shift in range(1, layers)]
    from_partner = [to_later(partner, shift) for shift in range(1, layers)]
    groups = far // 2
    piece = (2, groups, block, half_width)
    keep, *sends, stacked = pl.pallas_call(
        functools.partial(decode_body, dec_scale, layers),
        out_shape=(
            shape(piece, f32), shape(piece, bf16), shape(piece, bf16), shape(piece, bf16),
            shape((layers, row_count, feat_dev), bf16),
        ),
        scratch_shapes=[pltpu.VMEM((rows, half_width), f32)],
        name="decode",
    )(codes, partner, *from_own, *from_partner, dec_weight)
    others = swap_dp(halves)
    received = [swap_feat(send, s) for s, send in enumerate(sends, 1)]
    partial = call(add_body, "add", shape(piece, bf16), keep, *received)
    bit = 4
    while 2 * bit < count:
        partial = (partial.astype(f32) + swap_feat(partial, bit).astype(f32)).astype(bf16)
        bit *= 2
    local_errors = call(
        error_body, "errors", shape(piece, bf16), partial, swap_feat(partial, bit), targets, dec_bias
    )
    near_errors = [local_errors] + [swap_feat(local_errors, s) for s in range(1, 4)]
    errors, new_dec_bias, *terms = call(
        functools.partial(back_body, scale_rows, step_bias / row_count, layers),
        "back",
        (shape((row_count, half_width), bf16), shape((1, half_width), f32))
        + (shape((row_count, feat_dev), bf16),) * (layers - 1),
        *near_errors, dec_weight, dec_bias,
    )
    from_later = [
        lax.ppermute(term, "layer", [(i + shift, i) for i in range(layers - shift)])
        for shift, term in enumerate(terms, 1)
    ]
    term = call(
        functools.partial(own_body, scale_rows, layers),
        "own_term",
        shape((row_count, feat_dev), bf16),
        errors, dec_weight, *from_later,
    )
    other_term = swap_dp(term)
    new_dec_weight = pl.pallas_call(
        functools.partial(decoder_body, step_weight * scale_rows, layers),
        out_shape=shape(dec_weight.shape, bf16),
        grid=(layers, 1),
        in_specs=[
            pl.BlockSpec(stacked.shape, lambda i, j: (0, 0, 0)),
            pl.BlockSpec(errors.shape, lambda i, j: (0, 0)),
            pl.BlockSpec((1, 1, feat_dev, half_width), lambda i, j: (0, i, 0, 0)),
        ],
        out_specs=pl.BlockSpec((1, 1, feat_dev, half_width), lambda i, j: (0, i, 0, 0)),
        name="decoder_step",
    )(stacked, errors, dec_weight)
    new_enc_weight, new_enc_bias = call(
        functools.partial(encoder_body, step_weight * enc_scale),
        "encoder_step",
        (shape((1, width // 2, feat_dev), bf16), shape((1, feat_dev), f32)),
        *inputs, others, stacked, term, other_term, enc_weight, enc_bias,
    )
    return new_enc_weight, new_enc_bias, new_dec_weight, new_dec_bias


def general(resid, target, enc_weight, enc_bias, dec_weight, dec_bias):
    layer_count = lax.axis_size("layer")
    layer_index = lax.axis_index("layer")
    width = enc_weight.shape[1]
    feat_dev = enc_weight.shape[2]
    half_width = dec_weight.shape[3]
    enc_scale = width ** (-0.5)
    dec_scale = (feat_dev * lax.axis_size("feat")) ** (-0.5)
    inputs = lax.all_gather(resid[0], "feat", axis=1, tiled=True)
    preact = (
        enc_scale * jnp.dot(inputs, enc_weight[0], preferred_element_type=jnp.float32) + enc_bias[0]
    )
    codes = jnp.maximum(preact, 0.0).astype(jnp.bfloat16)
    token_codes = lax.all_gather(codes, "dp", axis=0, tiled=True)
    row_count = token_codes.shape[0]
    all_codes = lax.all_gather(token_codes[:, None, :], "layer", axis=1, tiled=True)
    scale_rows = dec_scale / row_count
    blocks = dec_weight[0]
    sources = jnp.arange(layer_count)
    alive = sources <= layer_index
    masked_codes = jnp.where(alive[None, :, None], all_codes, jnp.zeros((), jnp.bfloat16)).reshape(
        row_count, layer_count * feat_dev
    )
    flat_blocks = blocks.reshape(layer_count * feat_dev, half_width)
    summed = lax.psum_scatter(
        dec_scale * jnp.dot(masked_codes, flat_blocks, preferred_element_type=jnp.float32),
        "feat",
        scatter_dimension=0,
        tiled=True,
    )
    recon = summed + dec_bias[0]
    local_errors = (recon - target[0].astype(jnp.float32)).astype(jnp.bfloat16)
    errors = lax.all_gather(local_errors, "feat", axis=0, tiled=True)
    dec_grad = (scale_rows * contract_rows(masked_codes, errors)).reshape(
        layer_count, feat_dev, half_width
    )
    new_blocks = (blocks.astype(jnp.float32) - step_weight * dec_grad).astype(jnp.bfloat16)
    new_dec_bias = dec_bias[0] - step_bias * jnp.sum(errors.astype(jnp.float32), axis=0) / row_count
    terms = scale_rows * contract_width(errors, flat_blocks).reshape(
        row_count, layer_count, feat_dev
    )
    by_layer = lax.psum_scatter(
        terms * alive[None, :, None].astype(jnp.float32), "layer", scatter_dimension=1, tiled=True
    )
    code_grad = lax.psum_scatter(by_layer, "dp", scatter_dimension=0, tiled=True)[:, 0, :]
    pre_grad = jnp.where(preact > 0.0, code_grad, jnp.zeros_like(code_grad)).astype(jnp.bfloat16)
    enc_grad = enc_scale * contract_rows(inputs, pre_grad)
    bias_grad = jnp.sum(pre_grad.astype(jnp.float32), axis=0)
    dp_count = lax.axis_size("dp")
    dp_index = lax.axis_index("dp")
    share = width // dp_count
    enc_part = lax.psum_scatter(enc_grad, "dp", scatter_dimension=0, tiled=True)
    bias_total = lax.psum(bias_grad, "dp")
    old_part = lax.dynamic_slice_in_dim(enc_weight[0], dp_index * share, share, 0)
    new_enc = (old_part.astype(jnp.float32) - step_weight * enc_part).astype(jnp.bfloat16)
    new_enc_bias = enc_bias[0] - step_bias * bias_total
    return (new_enc[None], new_enc_bias[None], new_blocks[None], new_dec_bias[None])


def local(*operands):
    resid, target, enc_weight, _, dec_weight, _ = operands
    count = lax.axis_size("feat")
    fits = (
        lax.axis_size("dp") == 2
        and count >= 8
        and count & (count - 1) == 0
        and resid.shape[2] % 32 == 0
        and target.shape[1] % 32 == 0
        and enc_weight.shape[2] % 128 == 0
        and dec_weight.shape[3] % 128 == 0
    )
    return exchange(*operands) if fits else general(*operands)


def solution(mesh):
    placed = (
        P("layer", "dp", "feat"),
        P("layer", "feat", "dp"),
        P("layer", None, "feat"),
        P("layer", "feat"),
        P("layer", None, "feat", "dp"),
        P("layer", "dp"),
    )
    return jax.shard_map(
        local,
        mesh=mesh,
        in_specs=placed,
        out_specs=(
            P("layer", "dp", "feat"),
            P("layer", "feat"),
            P("layer", None, "feat", "dp"),
            P("layer", "dp"),
        ),
        check_vma=False,
    )
```
